32 devices in a mesh: head: 4 (over z), outer: 2 (over core), inner: 4 (over y, x).
Axes of the slice: x: 2, y: 2, z: 4, core: 2. Of those that a mesh axis runs over, the one named last changes fastest.
Arguments:
- query_in: bfloat16 [8, 384, 1024], P(('outer', 'inner'), 'head'), may hold values from -48 to 48
- key_in: bfloat16 [8, 384, 512], P(('outer', 'inner'), 'head'), may hold values from -6 to 6
- value_in: bfloat16 [8, 384, 512], P(('outer', 'inner'), 'head'), may hold values from -6 to 6
- grad_out: bfloat16 [8, 384, 1024], P(('outer', 'inner'), 'head'), may hold values from -48 to 48
Outputs:
- grad_query: bfloat16 [8, 384, 1024], P(('outer', 'inner'), 'head')
- grad_key: bfloat16 [8, 384, 512], P(('outer', 'inner'), 'head')
- grad_value: bfloat16 [8, 384, 512], P(('outer', 'inner'), 'head')
The draws below stay inside these ranges and needn't reach their ends.
All inputs are finite; a program needn't handle non-finite values.
Results may differ from the reference program's by a relative error of at most 0.0058.
Values may be sent and summed in bfloat16 or wider, within the bound.
A program may use at most 128 MiB of HBM per device.

```python
import jax
import jax.numpy as jnp
from jax import lax

HD = 128
GROUP = 2
WINDOW = 4096
T_DEV = 384
KV_HEADS = 4
Q_HEADS = 8
CTXB = 8


def draw_query_in(key, part):
    base_key = jax.random.fold_in(key, 11)
    mask_key = jax.random.fold_in(key, 12)
    size_key = jax.random.fold_in(key, 13)
    shape = (CTXB, T_DEV, Q_HEADS, HD)
    row_shape = (CTXB, T_DEV, Q_HEADS, 1)
    base = jax.random.normal(base_key, shape, jnp.float32) * 1.6
    spiked = jax.random.bernoulli(mask_key, 0.03, row_shape)
    factor = jnp.exp(jax.random.uniform(size_key, row_shape, jnp.float32, 1.7917595, 2.6390573))
    values = base * jnp.where(spiked, factor, 1.0)
    values = jnp.clip(values, -48.0, 48.0)
    return values.reshape(CTXB, T_DEV, Q_HEADS * HD).astype(jnp.bfloat16)


def shard_levels(rng, dims, cuts, least, top_value):
    gain = 1.0
    for position, shards_of in cuts:
        steps = jax.random.uniform(jax.random.fold_in(jax.random.fold_in(rng, 6), position), (shards_of,), jnp.float32, least / len(cuts), top_value / len(cuts))
        gain = gain * jnp.repeat(jnp.exp(steps), dims[position] // shards_of).reshape((-1,) + (1,) * (len(dims) - 1 - position))
    return gain


def bell_draw(stream_key, extent, scale, limit, split=(), kind=jnp.bfloat16):
    gain = shard_levels(stream_key, extent, split, -0.22, 0.18) if split else 1.0
    values = jax.random.normal(stream_key, extent, jnp.float32) * scale * gain
    return jnp.minimum(jnp.maximum(values, -limit), limit).astype(kind)


def setup_inputs(seed: int = 0) -> dict:
    key_list = jax.random.split(jax.random.key(seed), 5)
    return {
        "query_in": draw_query_in(jax.random.fold_in(key_list[4], 71), 0),
        "key_in": bell_draw(key_list[1], (CTXB, T_DEV, KV_HEADS * HD), 1.0, 6.0, ((0, 8), (1, 4))),
        "value_in": bell_draw(key_list[2], (CTXB, T_DEV, KV_HEADS * HD), 1.0, 6.0, ((0, 8), (1, 4))),
        "grad_out": bell_draw(key_list[3], (CTXB, T_DEV, Q_HEADS * HD), 8.0, 48.0, ((0, 8), (1, 4))),
    }


SOFT_CAP = 50.0
QUERY_SCALE = 1.0 / 12.0


def reference(query_in, key_in, value_in, grad_out):
    tok_rows = T_DEV
    lookback = (WINDOW + T_DEV - 2) // T_DEV
    key_span = (lookback + 1) * tok_rows
    all_rows = CTXB * tok_rows
    pad_rows = lookback * tok_rows
    query_all = query_in.reshape(all_rows, KV_HEADS, GROUP, HD)
    grad_all = grad_out.reshape(all_rows, KV_HEADS, GROUP, HD)
    key_all = jnp.concatenate([jnp.zeros((pad_rows, KV_HEADS, HD), key_in.dtype), key_in.reshape(all_rows, KV_HEADS, HD)], axis=0)
    value_all = jnp.concatenate([jnp.zeros((pad_rows, KV_HEADS, HD), value_in.dtype), value_in.reshape(all_rows, KV_HEADS, HD)], axis=0)

    def per_block(grad_sum, block_index):
        row_start = (block_index * tok_rows).astype(jnp.int32)
        query_blk = lax.dynamic_slice_in_dim(query_all, row_start, tok_rows, 0).astype(jnp.float32)
        grad_blk = lax.dynamic_slice_in_dim(grad_all, row_start, tok_rows, 0).astype(jnp.float32)
        key_blk = lax.dynamic_slice_in_dim(key_all, row_start, key_span, 0).astype(jnp.float32)
        value_blk = lax.dynamic_slice_in_dim(value_all, row_start, key_span, 0).astype(jnp.float32)
        scores = jnp.einsum("tagd,kad->agtk", query_blk, key_blk)
        capped = jnp.tanh(scores * (QUERY_SCALE / SOFT_CAP))
        grad_prob = jnp.einsum("tagd,kad->agtk", grad_blk, value_blk)
        grad_prob = lax.optimization_barrier(grad_prob.astype(jnp.bfloat16)).astype(jnp.float32)
        query_pos = row_start + lax.broadcasted_iota(jnp.int32, (tok_rows, key_span), 0)
        key_pos = row_start - pad_rows + lax.broadcasted_iota(jnp.int32, (tok_rows, key_span), 1)
        allowed = (key_pos <= query_pos) & (key_pos > query_pos - WINDOW) & (key_pos >= 0)
        weights = jnp.where(allowed, jnp.exp(SOFT_CAP * capped), 0.0)
        totals = jnp.sum(weights, axis=3)
        row_delta = jnp.sum(weights * grad_prob, axis=3) / totals
        attn_prob = weights / totals[..., None]
        prob_round = lax.optimization_barrier(attn_prob.astype(jnp.bfloat16)).astype(jnp.float32)
        grad_value = jnp.einsum("agtk,tagd->kad", prob_round, grad_blk)
        scaled = attn_prob * (grad_prob - row_delta[..., None]) * (QUERY_SCALE * (1.0 - capped * capped))
        scaled = lax.optimization_barrier(scaled.astype(jnp.bfloat16)).astype(jnp.float32)
        grad_query = jnp.einsum("agtk,kad->tagd", scaled, key_blk)
        grad_key = jnp.einsum("agtk,tagd->kad", scaled, query_blk)
        kv_grads = jnp.stack([grad_key, grad_value], axis=2)
        current = lax.dynamic_slice_in_dim(grad_sum, row_start, key_span, 0)
        grad_sum = lax.dynamic_update_slice_in_dim(grad_sum, current + kv_grads, row_start, 0)
        return grad_sum, grad_query

    grad_init = jnp.zeros((pad_rows + all_rows, KV_HEADS, 2, HD), jnp.float32)
    grad_sum, query_grads = lax.scan(per_block, grad_init, jnp.arange(CTXB, dtype=jnp.int32))
    grad_query = query_grads.reshape(CTXB, tok_rows, Q_HEADS * HD).astype(jnp.bfloat16)
    grad_key = grad_sum[pad_rows:, :, 0].reshape(CTXB, tok_rows, KV_HEADS * HD).astype(jnp.bfloat16)
    grad_value = grad_sum[pad_rows:, :, 1].reshape(CTXB, tok_rows, KV_HEADS * HD).astype(jnp.bfloat16)
    return (grad_query, grad_key, grad_value)
```

```python
import functools

import jax
import jax.numpy as jnp
from jax import lax
from jax.experimental import pallas as pl
from jax.experimental.pallas import tpu as pltpu
from jax.sharding import PartitionSpec as P

HD = 128
GROUP = 2
WINDOW = 4096
SOFT_CAP = 50.0
QUERY_SCALE = 1.0 / 12.0
MESH = pl.DeviceIdType.MESH
KT = 128


def dot(a, b, ca, cb):
    return lax.dot_general(a, b, (((ca,), (cb,)), ((), ())), preferred_element_type=jnp.float32)


def kernel(
    heads, outer_n, inner_n, back,
    q_in, k_in, v_in, g_in,
    q_out, k_out, v_out,
    qs, gs, qst, gst, kv, e_all, c_all, d_all, tot, wgt, pb, sc, dqt, dq, dkv, dsend, drecv, own,
    a_send, a_recv, a_loc, b_send, b_recv, d_ssem, d_rsem, e_send, e_recv, e_loc,
):
    rows = q_in.shape[0]
    tok = rows * heads
    ctx = outer_n * inner_n
    h = lax.axis_index("head")
    pos = lax.axis_index("outer") * inner_n + lax.axis_index("inner")

    def at(t):
        return {"outer": lax.div(t, inner_n), "inner": lax.rem(t, inner_n)}

    def head_at(d):
        return lax.rem(h + d, heads)

    def part(who):
        return pl.ds(pl.multiple_of(who * rows, rows), rows)

    def lanes(who, width):
        return pl.ds(pl.multiple_of(who * width, width), width)

    barrier = pltpu.get_barrier_semaphore()
    for d in range(1, heads):
        pl.semaphore_signal(barrier, inc=1, device_id={"head": head_at(d)}, device_id_type=MESH)
    for s in range(1, back + 1):
        @pl.when(pos + s < ctx)
        def _():
            pl.semaphore_signal(barrier, inc=1, device_id=at(pos + s), device_id_type=MESH)

        @pl.when(pos - s >= 0)
        def _():
            pl.semaphore_signal(barrier, inc=1, device_id=at(pos - s), device_id_type=MESH)
    peers = heads - 1 + jnp.minimum(pos, back) + jnp.minimum(ctx - 1 - pos, back)
    pl.semaphore_wait(barrier, peers)

    srcs = ((k_in, HD), (v_in, HD), (q_in, GROUP * HD), (g_in, GROUP * HD))

    def dst_a(kind, who):
        if kind < 2:
            return kv.at[0, kind, part(who)]
        return (qs if kind == 2 else gs).at[part(who)]

    def copy_a(kind, d):
        ref, width = srcs[kind]
        return pltpu.make_async_remote_copy(
            src_ref=ref.at[:, lanes(head_at(d), width)],
            dst_ref=dst_a(kind, h),
            send_sem=a_send.at[kind, d], recv_sem=a_recv.at[kind, d],
            device_id={"head": head_at(d)}, device_id_type=MESH,
        )

    def arrival_a(kind, d):
        ref, width = srcs[kind]
        return pltpu.make_async_remote_copy(
            src_ref=ref.at[:, lanes(h, width)],
            dst_ref=dst_a(kind, head_at(heads - d)),
            send_sem=a_send.at[kind, d], recv_sem=a_recv.at[kind, d],
            device_id={"head": head_at(d)}, device_id_type=MESH,
        )

    def local_a(kind):
        ref, width = srcs[kind]
        return pltpu.make_async_copy(ref.at[:, lanes(h, width)], dst_a(kind, h), a_loc.at[kind])

    for kind in (0, 1):
        local_a(kind).start()
    for kind in (0, 1, 2, 3):
        for d in range(1, heads):
            copy_a(kind, d).start()
    for kind in (2, 3):
        local_a(kind).start()

    def copy_b(s, d):
        who = part(head_at(heads - d))
        return pltpu.make_async_remote_copy(
            src_ref=kv.at[0, :, who], dst_ref=kv.at[s, :, who],
            send_sem=b_send.at[s, d], recv_sem=b_recv.at[s, d],
            device_id=at(lax.rem(pos + s, ctx)), device_id_type=MESH,
        )

    for d in range(heads):
        for kind in (0, 1):
            if d == 0:
                local_a(kind).wait()
            else:
                arrival_a(kind, d).wait_recv()
        for s in range(1, back + 1):
            @pl.when(pos + s < ctx)
            def _():
                copy_b(s, d).start()

    for kind in (2, 3):
        local_a(kind).wait()
        for d in range(1, heads):
            arrival_a(kind, d).wait_recv()
    for j in range(GROUP):
        qst[j * tok:(j + 1) * tok] = qs[:, j * HD:(j + 1) * HD]
        gst[j * tok:(j + 1) * tok] = gs[:, j * HD:(j + 1) * HD]
    tot[...] = jnp.zeros_like(tot)
    wgt[...] = jnp.zeros_like(wgt)
    dqt[...] = jnp.zeros_like(dqt)

    free = (WINDOW - tok) // tok

    def first(s, masked):
        for t in range(tok // KT):
            at_t = slice(t * KT, (t + 1) * KT)
            keys = kv[s, 0, at_t]
            vals = kv[s, 1, at_t]
            for j in range(GROUP):
                col = slice(j * tok, (j + 1) * tok)
                capped = jnp.tanh(dot(keys, qst[col], 1, 1) * (QUERY_SCALE / SOFT_CAP))
                e = jnp.exp(SOFT_CAP * capped)
                if masked:
                    apart = (
                        s * tok - t * KT
                        + lax.broadcasted_iota(jnp.int32, e.shape, 1)
                        - lax.broadcasted_iota(jnp.int32, e.shape, 0)
                    )
                    e = jnp.where((apart >= 0) & (apart < WINDOW), e, 0.0)
                dp = dot(vals, gst[col], 1, 1).astype(jnp.bfloat16)
                c_all[s, at_t, col] = capped
                e_all[s, at_t, col] = e
                d_all[s, at_t, col] = dp
                tot[:, col] += jnp.sum(e.reshape(KT // 8, 8, tok), axis=0)
                wgt[:, col] += jnp.sum((e * dp.astype(jnp.float32)).reshape(KT // 8, 8, tok), axis=0)

    first(0, True)
    reach = jnp.minimum(pos, back)

    def first_step(masked, s, carry):
        for d in range(heads):
            copy_b(s, d).wait_recv()
        first(s, masked)
        return carry

    edge = jnp.minimum(reach, free)
    lax.fori_loop(1, edge + 1, functools.partial(first_step, False), 0)
    if back > free:
        lax.fori_loop(edge + 1, reach + 1, functools.partial(first_step, True), 0)

    total = jnp.sum(tot[...], axis=0, keepdims=True)
    inv = 1.0 / total
    delta = jnp.sum(wgt[...], axis=0, keepdims=True) * inv
    tot[0:1] = inv
    wgt[0:1] = delta

    def second(s):
        for t in range(tok // KT):
            at_t = slice(t * KT, (t + 1) * KT)
            for j in range(GROUP):
                col = slice(j * tok, (j + 1) * tok)
                capped = c_all[s, at_t, col]
                prob = e_all[s, at_t, col] * tot[0:1, col]
                pb[at_t, col] = prob.astype(jnp.bfloat16)
                diff = d_all[s, at_t, col].astype(jnp.float32) - wgt[0:1, col]
                sc[at_t, col] = (
                    prob * diff * (QUERY_SCALE - QUERY_SCALE * (capped * capped))
                ).astype(jnp.bfloat16)
        scaled = sc[...]
        dqt[...] += dot(kv[s, 0], scaled, 0, 0)
        return dot(scaled, qst[...], 1, 0), dot(pb[...], gst[...], 1, 0)

    def copy_d(s):
        return pltpu.make_async_remote_copy(
            src_ref=dsend.at[s - 1], dst_ref=drecv.at[s - 1],
            send_sem=d_ssem.at[s - 1], recv_sem=d_rsem.at[s - 1],
            device_id=at(lax.rem(pos - s + ctx, ctx)), device_id_type=MESH,
        )

    def second_step(i, carry):
        s = reach - i
        dk, dv = second(s)
        dsend[s - 1, 0] = dk.astype(jnp.bfloat16)
        dsend[s - 1, 1] = dv.astype(jnp.bfloat16)
        copy_d(s).start()
        return carry

    lax.fori_loop(0, reach, second_step, 0)
    dk, dv = second(0)
    own[0] = dk
    own[1] = dv
    for j in range(GROUP):
        dq[:, j * HD:(j + 1) * HD] = dqt[:, j * tok:(j + 1) * tok].T.astype(jnp.bfloat16)

    outs = ((q_out, GROUP * HD), (k_out, HD), (v_out, HD))

    def src_e(kind, who):
        return dq.at[part(who)] if kind == 0 else dkv.at[kind - 1, part(who)]

    def copy_e(kind, d):
        ref, width = outs[kind]
        return pltpu.make_async_remote_copy(
            src_ref=src_e(kind, head_at(d)), dst_ref=ref.at[:, lanes(h, width)],
            send_sem=e_send.at[kind, d], recv_sem=e_recv.at[kind, d],
            device_id={"head": head_at(d)}, device_id_type=MESH,
        )

    def arrival_e(kind, d):
        ref, width = outs[kind]
        return pltpu.make_async_remote_copy(
            src_ref=src_e(kind, h), dst_ref=ref.at[:, lanes(head_at(heads - d), width)],
            send_sem=e_send.at[kind, d], recv_sem=e_recv.at[kind, d],
            device_id={"head": head_at(d)}, device_id_type=MESH,
        )

    def local_e(kind):
        ref, width = outs[kind]
        return pltpu.make_async_copy(src_e(kind, h), ref.at[:, lanes(h, width)], e_loc.at[kind])

    for d in range(1, heads):
        copy_e(0, d).start()
    local_e(0).start()

    def collect(s, carry):
        copy_d(s).wait_recv()
        own[...] += drecv[s - 1].astype(jnp.float32)
        return carry

    lax.fori_loop(1, jnp.minimum(ctx - 1 - pos, back) + 1, collect, 0)
    dkv[...] = own[...].astype(jnp.bfloat16)
    for kind in (1, 2):
        for d in range(1, heads):
            copy_e(kind, d).start()
        local_e(kind).start()

    for kind in range(4):
        for d in range(1, heads):
            copy_a(kind, d).wait_send()

    def sent_b(s, carry):
        for d in range(heads):
            copy_b(s, d).wait_send()
        return carry

    lax.fori_loop(1, jnp.minimum(ctx - 1 - pos, back) + 1, sent_b, 0)

    def sent_d(s, carry):
        copy_d(s).wait_send()
        return carry

    lax.fori_loop(1, reach + 1, sent_d, 0)
    for kind in range(3):
        local_e(kind).wait()
        for d in range(1, heads):
            copy_e(kind, d).wait_send()
            arrival_e(kind, d).wait_recv()


def solution(mesh):
    heads, outer_n, inner_n = (mesh.shape[a] for a in ("head", "outer", "inner"))

    def body(query_in, key_in, value_in, grad_out):
        rows = query_in.shape[1]
        tok = rows * heads
        back = min((WINDOW + tok - 2) // tok, outer_n * inner_n - 1)
        wide = GROUP * tok
        bf16, f32 = jnp.bfloat16, jnp.float32
        sem = pltpu.SemaphoreType.DMA
        shapes = [(query_in.shape[1:]), (key_in.shape[1:]), (value_in.shape[1:])]
        res = pl.pallas_call(
            functools.partial(kernel, heads, outer_n, inner_n, back),
            out_shape=[jax.ShapeDtypeStruct(s, bf16) for s in shapes],
            in_specs=[pl.BlockSpec(memory_space=pltpu.VMEM)] * 4,
            out_specs=[pl.BlockSpec(memory_space=pltpu.VMEM)] * 3,
            scratch_shapes=[
                pltpu.VMEM((tok, GROUP * HD), bf16),
                pltpu.VMEM((tok, GROUP * HD), bf16),
                pltpu.VMEM((wide, HD), bf16),
                pltpu.VMEM((wide, HD), bf16),
                pltpu.VMEM((back + 1, 2, tok, HD), bf16),
                pltpu.VMEM((back + 1, tok, wide), f32),
                pltpu.VMEM((back + 1, tok, wide), f32),
                pltpu.VMEM((back + 1, tok, wide), bf16),
                pltpu.VMEM((8, wide), f32),
                pltpu.VMEM((8, wide), f32),
                pltpu.VMEM((tok, wide), bf16),
                pltpu.VMEM((tok, wide), bf16),
                pltpu.VMEM((HD, wide), f32),
                pltpu.VMEM((tok, GROUP * HD), bf16),
                pltpu.VMEM((2, tok, HD), bf16),
                pltpu.VMEM((back, 2, tok, HD), bf16),
                pltpu.VMEM((back, 2, tok, HD), bf16),
                pltpu.VMEM((2, tok, HD), f32),
                sem((4, heads)), sem((4, heads)), sem((4,)),
                sem((back + 1, heads)), sem((back + 1, heads)),
                sem((back,)), sem((back,)),
                sem((3, heads)), sem((3, heads)), sem((3,)),
            ],
            compiler_params=pltpu.CompilerParams(
                collective_id=0, has_side_effects=True, vmem_limit_bytes=60 * 1024 * 1024
            ),
        )(query_in[0], key_in[0], value_in[0], grad_out[0])
        return tuple(r[None] for r in res)

    spec = P(("outer", "inner"), "head", None)
    return jax.shard_map(
        body, mesh=mesh, in_specs=(spec,) * 4, out_specs=(spec,) * 3, check_vma=False
    )
```

```python
import functools

import jax
import jax.numpy as jnp
from jax import lax
from jax.experimental import pallas as pl
from jax.experimental.pallas import tpu as pltpu
from jax.sharding import PartitionSpec as P

HD = 128
GROUP = 2
WINDOW = 4096
SOFT_CAP = 50.0
QUERY_SCALE = 1.0 / 12.0
MESH = pl.DeviceIdType.MESH
KT = 128


def dot(a, b, ca, cb):
    return lax.dot_general(a, b, (((ca,), (cb,)), ((), ())), preferred_element_type=jnp.float32)


def kernel(
    heads, outer_n, inner_n, back,
    q_in, k_in, v_in, g_in,
    q_out, k_out, v_out,
    qs, gs, qst, gst, kv, e_all, c_all, d_all, tot, wgt, pb, sc, dqt, dq, dkv, dsend, drecv, own,
    a_send, a_recv, a_loc, b_send, b_recv, d_ssem, d_rsem, e_send, e_recv, e_loc,
):
    rows = q_in.shape[0]
    tok = rows * heads
    ctx = outer_n * inner_n
    h = lax.axis_index("head")
    pos = lax.axis_index("outer") * inner_n + lax.axis_index("inner")

    def at(t):
        return {"outer": lax.div(t, inner_n), "inner": lax.rem(t, inner_n)}

    def head_at(d):
        return lax.rem(h + d, heads)

    def part(who):
        return pl.ds(pl.multiple_of(who * rows, rows), rows)

    def lanes(who, width):
        return pl.ds(pl.multiple_of(who * width, width), width)

    barrier = pltpu.get_barrier_semaphore()
    for d in range(1, heads):
        pl.semaphore_signal(barrier, inc=1, device_id={"head": head_at(d)}, device_id_type=MESH)
    for s in range(1, back + 1):
        @pl.when(pos + s < ctx)
        def _():
            pl.semaphore_signal(barrier, inc=1, device_id=at(pos + s), device_id_type=MESH)

        @pl.when(pos - s >= 0)
        def _():
            pl.semaphore_signal(barrier, inc=1, device_id=at(pos - s), device_id_type=MESH)
    peers = heads - 1 + jnp.minimum(pos, back) + jnp.minimum(ctx - 1 - pos, back)
    pl.semaphore_wait(barrier, peers)

    srcs = ((k_in, HD), (v_in, HD), (q_in, GROUP * HD), (g_in, GROUP * HD))

    def dst_a(kind, who):
        if kind < 2:
            return kv.at[0, kind, part(who)]
        return (qs if kind == 2 else gs).at[part(who)]

    def copy_a(kind, d):
        ref, width = srcs[kind]
        return pltpu.make_async_remote_copy(
            src_ref=ref.at[:, lanes(head_at(d), width)],
            dst_ref=dst_a(kind, h),
            send_sem=a_send.at[kind, d], recv_sem=a_recv.at[kind, d],
            device_id={"head": head_at(d)}, device_id_type=MESH,
        )

    def arrival_a(kind, d):
        ref, width = srcs[kind]
        return pltpu.make_async_remote_copy(
            src_ref=ref.at[:, lanes(h, width)],
            dst_ref=dst_a(kind, head_at(heads - d)),
            send_sem=a_send.at[kind, d], recv_sem=a_recv.at[kind, d],
            device_id={"head": head_at(d)}, device_id_type=MESH,
        )

    def local_a(kind):
        ref, width = srcs[kind]
        return pltpu.make_async_copy(ref.at[:, lanes(h, width)], dst_a(kind, h), a_loc.at[kind])

    for kind in (0, 1):
        local_a(kind).start()
    for kind in (0, 1, 2, 3):
        for d in range(1, heads):
            copy_a(kind, d).start()
    for kind in (2, 3):
        local_a(kind).start()

    def copy_b(s, d):
        who = part(head_at(heads - d))
        return pltpu.make_async_remote_copy(
            src_ref=kv.at[0, :, who], dst_ref=kv.at[s, :, who],
            send_sem=b_send.at[s, d], recv_sem=b_recv.at[s, d],
            device_id=at(lax.rem(pos + s, ctx)), device_id_type=MESH,
        )

    for d in range(heads):
        for kind in (0, 1):
            if d == 0:
                local_a(kind).wait()
            else:
                arrival_a(kind, d).wait_recv()
        for s in range(1, back + 1):
            @pl.when(pos + s < ctx)
            def _():
                copy_b(s, d).start()

    tot[...] = jnp.zeros_like(tot)
    wgt[...] = jnp.zeros_like(wgt)
    dqt[...] = jnp.zeros_like(dqt)

    free = (WINDOW - tok) // tok

    def first(s, masked):
        for t in range(tok // KT):
            at_t = slice(t * KT, (t + 1) * KT)
            keys = kv[s, 0, at_t]
            for j in range(GROUP):
                col = slice(j * tok, (j + 1) * tok)
                capped = jnp.tanh(dot(keys, qst[col], 1, 1) * (QUERY_SCALE / SOFT_CAP))
                e = jnp.exp(SOFT_CAP * capped)
                if masked:
                    apart = (
                        s * tok - t * KT
                        + lax.broadcasted_iota(jnp.int32, e.shape, 1)
                        - lax.broadcasted_iota(jnp.int32, e.shape, 0)
                    )
                    e = jnp.where((apart >= 0) & (apart < WINDOW), e, 0.0)
                c_all[s, at_t, col] = capped
                e_all[s, at_t, col] = e
                tot[:, col] += jnp.sum(e.reshape(KT // 8, 8, tok), axis=0)

    def first_dp(s, carry):
        for t in range(tok // KT):
            at_t = slice(t * KT, (t + 1) * KT)
            vals = kv[s, 1, at_t]
            for j in range(GROUP):
                col = slice(j * tok, (j + 1) * tok)
                dp = dot(vals, gst[col], 1, 1).astype(jnp.bfloat16)
                d_all[s, at_t, col] = dp
                weighted = e_all[s, at_t, col] * dp.astype(jnp.float32)
                wgt[:, col] += jnp.sum(weighted.reshape(KT // 8, 8, tok), axis=0)
        return carry

    def take(kind, whole, stacked):
        local_a(kind).wait()
        for d in range(1, heads):
            arrival_a(kind, d).wait_recv()
        for j in range(GROUP):
            stacked[j * tok:(j + 1) * tok] = whole[:, j * HD:(j + 1) * HD]

    take(2, qs, qst)
    first(0, True)
    reach = jnp.minimum(pos, back)

    def first_step(masked, s, carry):
        for d in range(heads):
            copy_b(s, d).wait_recv()
        first(s, masked)
        return carry

    edge = jnp.minimum(reach, free)
    lax.fori_loop(1, edge + 1, functools.partial(first_step, False), 0)
    if back > free:
        lax.fori_loop(edge + 1, reach + 1, functools.partial(first_step, True), 0)
    take(3, gs, gst)
    lax.fori_loop(0, reach + 1, first_dp, 0)

    total = jnp.sum(tot[...], axis=0, keepdims=True)
    inv = 1.0 / total
    delta = jnp.sum(wgt[...], axis=0, keepdims=True) * inv
    tot[0:1] = inv
    wgt[0:1] = delta

    def second(s):
        dks, dvs = [], []
        for t in range(tok // KT):
            at_t = slice(t * KT, (t + 1) * KT)
            probs, scs = [], []
            for j in range(GROUP):
                col = slice(j * tok, (j + 1) * tok)
                capped = c_all[s, at_t, col]
                prob = e_all[s, at_t, col] * tot[0:1, col]
                diff = d_all[s, at_t, col].astype(jnp.float32) - wgt[0:1, col]
                probs.append(prob.astype(jnp.bfloat16))
                scs.append(
                    (prob * diff * (QUERY_SCALE - QUERY_SCALE * (capped * capped))).astype(jnp.bfloat16)
                )
            scaled = jnp.concatenate(scs, axis=1)
            dvs.append(dot(jnp.concatenate(probs, axis=1), gst[...], 1, 0))
            dks.append(dot(scaled, qst[...], 1, 0))
            dqt[...] += dot(kv[s, 0, at_t], scaled, 0, 0)
        return jnp.concatenate(dks, axis=0), jnp.concatenate(dvs, axis=0)

    def copy_d(s):
        return pltpu.make_async_remote_copy(
            src_ref=dsend.at[s - 1], dst_ref=drecv.at[s - 1],
            send_sem=d_ssem.at[s - 1], recv_sem=d_rsem.at[s - 1],
            device_id=at(lax.rem(pos - s + ctx, ctx)), device_id_type=MESH,
        )

    def second_step(i, carry):
        s = reach - i
        dk, dv = second(s)
        dsend[s - 1, 0] = dk.astype(jnp.bfloat16)
        dsend[s - 1, 1] = dv.astype(jnp.bfloat16)
        copy_d(s).start()
        return carry

    lax.fori_loop(0, reach, second_step, 0)
    dk, dv = second(0)
    own[0] = dk
    own[1] = dv
    for j in range(GROUP):
        dq[:, j * HD:(j + 1) * HD] = dqt[:, j * tok:(j + 1) * tok].T.astype(jnp.bfloat16)

    outs = ((q_out, GROUP * HD), (k_out, HD), (v_out, HD))

    def src_e(kind, who):
        return dq.at[part(who)] if kind == 0 else dkv.at[kind - 1, part(who)]

    def copy_e(kind, d):
        ref, width = outs[kind]
        return pltpu.make_async_remote_copy(
            src_ref=src_e(kind, head_at(d)), dst_ref=ref.at[:, lanes(h, width)],
            send_sem=e_send.at[kind, d], recv_sem=e_recv.at[kind, d],
            device_id={"head": head_at(d)}, device_id_type=MESH,
        )

    def arrival_e(kind, d):
        ref, width = outs[kind]
        return pltpu.make_async_remote_copy(
            src_ref=src_e(kind, h), dst_ref=ref.at[:, lanes(head_at(heads - d), width)],
            send_sem=e_send.at[kind, d], recv_sem=e_recv.at[kind, d],
            device_id={"head": head_at(d)}, device_id_type=MESH,
        )

    def local_e(kind):
        ref, width = outs[kind]
        return pltpu.make_async_copy(src_e(kind, h), ref.at[:, lanes(h, width)], e_loc.at[kind])

    for d in range(1, heads):
        copy_e(0, d).start()
    local_e(0).start()

    def collect(s, carry):
        copy_d(s).wait_recv()
        own[...] += drecv[s - 1].astype(jnp.float32)
        return carry

    lax.fori_loop(1, jnp.minimum(ctx - 1 - pos, back) + 1, collect, 0)
    dkv[...] = own[...].astype(jnp.bfloat16)
    for kind in (1, 2):
        for d in range(1, heads):
            copy_e(kind, d).start()
        local_e(kind).start()

    for kind in range(4):
        for d in range(1, heads):
            copy_a(kind, d).wait_send()

    def sent_b(s, carry):
        for d in range(heads):
            copy_b(s, d).wait_send()
        return carry

    lax.fori_loop(1, jnp.minimum(ctx - 1 - pos, back) + 1, sent_b, 0)

    def sent_d(s, carry):
        copy_d(s).wait_send()
        return carry

    lax.fori_loop(1, reach + 1, sent_d, 0)
    for kind in range(3):
        local_e(kind).wait()
        for d in range(1, heads):
            copy_e(kind, d).wait_send()
            arrival_e(kind, d).wait_recv()


def hand_on(a, b, c, a_to, b_to, c_to, a_via, b_via, c_via, sems):
    ways = ((a, a_via, a_to), (b, b_via, b_to), (c, c_via, c_to))
    into = [pltpu.make_async_copy(x, v, sems.at[0, i]) for i, (x, v, _) in enumerate(ways)]
    out = [pltpu.make_async_copy(v, y, sems.at[1, i]) for i, (_, v, y) in enumerate(ways)]
    for copy in into:
        copy.start()
    for before, after in zip(into, out):
        before.wait()
        after.start()
    for copy in out:
        copy.wait()


def solution(mesh):
    heads, outer_n, inner_n = (mesh.shape[a] for a in ("head", "outer", "inner"))

    def body(query_in, key_in, value_in, grad_out):
        rows = query_in.shape[1]
        tok = rows * heads
        back = min((WINDOW + tok - 2) // tok, outer_n * inner_n - 1)
        wide = GROUP * tok
        bf16, f32 = jnp.bfloat16, jnp.float32
        sem = pltpu.SemaphoreType.DMA
        shapes = [(query_in.shape[1:]), (key_in.shape[1:]), (value_in.shape[1:])]
        res = pl.pallas_call(
            functools.partial(kernel, heads, outer_n, inner_n, back),
            out_shape=[jax.ShapeDtypeStruct(s, bf16) for s in shapes],
            in_specs=[pl.BlockSpec(memory_space=pl.ANY)] * 4,
            out_specs=[pl.BlockSpec(memory_space=pl.ANY)] * 3,
            scratch_shapes=[
                pltpu.VMEM((tok, GROUP * HD), bf16),
                pltpu.VMEM((tok, GROUP * HD), bf16),
                pltpu.VMEM((wide, HD), bf16),
                pltpu.VMEM((wide, HD), bf16),
                pltpu.VMEM((back + 1, 2, tok, HD), bf16),
                pltpu.VMEM((back + 1, tok, wide), f32),
                pltpu.VMEM((back + 1, tok, wide), f32),
                pltpu.VMEM((back + 1, tok, wide), bf16),
                pltpu.VMEM((8, wide), f32),
                pltpu.VMEM((8, wide), f32),
                pltpu.VMEM((tok, wide), bf16),
                pltpu.VMEM((tok, wide), bf16),
                pltpu.VMEM((HD, wide), f32),
                pltpu.VMEM((tok, GROUP * HD), bf16),
                pltpu.VMEM((2, tok, HD), bf16),
                pltpu.VMEM((back, 2, tok, HD), bf16),
                pltpu.VMEM((back, 2, tok, HD), bf16),
                pltpu.VMEM((2, tok, HD), f32),
                sem((4, heads)), sem((4, heads)), sem((4,)),
                sem((back + 1, heads)), sem((back + 1, heads)),
                sem((back,)), sem((back,)),
                sem((3, heads)), sem((3, heads)), sem((3,)),
            ],
            compiler_params=pltpu.CompilerParams(
                collective_id=0, has_side_effects=True, vmem_limit_bytes=60 * 1024 * 1024
            ),
        )(query_in[0], key_in[0], value_in[0], grad_out[0])
        res = pl.pallas_call(
            hand_on,
            out_shape=[jax.ShapeDtypeStruct(s, bf16) for s in shapes],
            in_specs=[pl.BlockSpec(memory_space=pl.ANY)] * 3,
            out_specs=[pl.BlockSpec(memory_space=pl.ANY)] * 3,
            scratch_shapes=[pltpu.VMEM(s, bf16) for s in shapes] + [sem((2, 3))],
        )(*res)
        return tuple(r[None] for r in res)

    spec = P(("outer", "inner"), "head", None)
    return jax.shard_map(
        body, mesh=mesh, in_specs=(spec,) * 4, out_specs=(spec,) * 3, check_vma=False
    )
```

```python
import functools

import jax
import jax.numpy as jnp
from jax import lax
from jax.experimental import pallas as pl
from jax.experimental.pallas import tpu as pltpu
from jax.sharding import PartitionSpec as P

HD = 128
GROUP = 2
WINDOW = 4096
SOFT_CAP = 50.0
QUERY_SCALE = 1.0 / 12.0
MESH = pl.DeviceIdType.MESH
KT = 128


def dot(a, b, ca, cb):
    return lax.dot_general(a, b, (((ca,), (cb,)), ((), ())), preferred_element_type=jnp.float32)


def kernel(
    heads, outer_n, inner_n, back,
    q_in, k_in, v_in, g_in,
    q_out, k_out, v_out,
    qs, gs, qst, gst, kv, e_all, c_all, d_all, tot, wgt, pb, sc, dqt, dq, dkv, dsend, drecv, own,
    a_send, a_recv, a_loc, b_send, b_recv, d_ssem, d_rsem, e_send, e_recv, e_loc,
):
    rows = q_in.shape[0]
    tok = rows * heads
    ctx = outer_n * inner_n
    h = lax.axis_index("head")
    pos = lax.axis_index("outer") * inner_n + lax.axis_index("inner")

    def at(t):
        return {"outer": lax.div(t, inner_n), "inner": lax.rem(t, inner_n)}

    def head_at(d):
        return lax.rem(h + d, heads)

    def part(who):
        return pl.ds(pl.multiple_of(who * rows, rows), rows)

    def lanes(who, width):
        return pl.ds(pl.multiple_of(who * width, width), width)

    barrier = pltpu.get_barrier_semaphore()
    for d in range(1, heads):
        pl.semaphore_signal(barrier, inc=1, device_id={"head": head_at(d)}, device_id_type=MESH)
    for s in range(1, back + 1):
        @pl.when(pos + s < ctx)
        def _():
            pl.semaphore_signal(barrier, inc=1, device_id=at(pos + s), device_id_type=MESH)

        @pl.when(pos - s >= 0)
        def _():
            pl.semaphore_signal(barrier, inc=1, device_id=at(pos - s), device_id_type=MESH)
    peers = heads - 1 + jnp.minimum(pos, back) + jnp.minimum(ctx - 1 - pos, back)
    pl.semaphore_wait(barrier, peers)

    srcs = ((k_in, HD), (v_in, HD), (q_in, GROUP * HD), (g_in, GROUP * HD))

    def dst_a(kind, who):
        if kind < 2:
            return kv.at[0, kind, part(who)]
        return (qs if kind == 2 else gs).at[part(who)]

    def copy_a(kind, d):
        ref, width = srcs[kind]
        return pltpu.make_async_remote_copy(
            src_ref=ref.at[:, lanes(head_at(d), width)],
            dst_ref=dst_a(kind, h),
            send_sem=a_send.at[kind, d], recv_sem=a_recv.at[kind, d],
            device_id={"head": head_at(d)}, device_id_type=MESH,
        )

    def arrival_a(kind, d):
        ref, width = srcs[kind]
        return pltpu.make_async_remote_copy(
            src_ref=ref.at[:, lanes(h, width)],
            dst_ref=dst_a(kind, head_at(heads - d)),
            send_sem=a_send.at[kind, d], recv_sem=a_recv.at[kind, d],
            device_id={"head": head_at(d)}, device_id_type=MESH,
        )

    def local_a(kind):
        ref, width = srcs[kind]
        return pltpu.make_async_copy(ref.at[:, lanes(h, width)], dst_a(kind, h), a_loc.at[kind])

    for kind in (0, 1):
        local_a(kind).start()
    for kind in (0, 1, 2, 3):
        for d in range(1, heads):
            copy_a(kind, d).start()
    for kind in (2, 3):
        local_a(kind).start()

    def copy_b(s, d):
        who = part(head_at(heads - d))
        return pltpu.make_async_remote_copy(
            src_ref=kv.at[0, :, who], dst_ref=kv.at[s, :, who],
            send_sem=b_send.at[s, d], recv_sem=b_recv.at[s, d],
            device_id=at(lax.rem(pos + s, ctx)), device_id_type=MESH,
        )

    for d in range(heads):
        for kind in (0, 1):
            if d == 0:
                local_a(kind).wait()
            else:
                arrival_a(kind, d).wait_recv()
        for s in range(1, back + 1):
            @pl.when(pos + s < ctx)
            def _():
                copy_b(s, d).start()

    tot[...] = jnp.zeros_like(tot)
    wgt[...] = jnp.zeros_like(wgt)
    dqt[...] = jnp.zeros_like(dqt)

    free = (WINDOW - tok) // tok

    def first(s, masked):
        for t in range(tok // KT):
            at_t = slice(t * KT, (t + 1) * KT)
            keys = kv[s, 0, at_t]
            for j in range(GROUP):
                col = slice(j * tok, (j + 1) * tok)
                capped = jnp.tanh(dot(keys, qst[col], 1, 1) * (QUERY_SCALE / SOFT_CAP))
                e = jnp.exp(SOFT_CAP * capped)
                if masked:
                    apart = (
                        s * tok - t * KT
                        + lax.broadcasted_iota(jnp.int32, e.shape, 1)
                        - lax.broadcasted_iota(jnp.int32, e.shape, 0)
                    )
                    e = jnp.where((apart >= 0) & (apart < WINDOW), e, 0.0)
                c_all[s, at_t, col] = capped
                e_all[s, at_t, col] = e
                tot[:, col] += jnp.sum(e.reshape(KT // 8, 8, tok), axis=0)

    def copy_d(s, which):
        return pltpu.make_async_remote_copy(
            src_ref=dsend.at[s - 1, which], dst_ref=drecv.at[s - 1, which],
            send_sem=d_ssem.at[s - 1, which], recv_sem=d_rsem.at[s - 1, which],
            device_id=at(lax.rem(pos - s + ctx, ctx)), device_id_type=MESH,
        )

    def first_dp(s):
        dvs = []
        for t in range(tok // KT):
            at_t = slice(t * KT, (t + 1) * KT)
            vals = kv[s, 1, at_t]
            probs = []
            for j in range(GROUP):
                col = slice(j * tok, (j + 1) * tok)
                dp = dot(vals, gst[col], 1, 1).astype(jnp.bfloat16)
                d_all[s, at_t, col] = dp
                e = e_all[s, at_t, col]
                weighted = e * dp.astype(jnp.float32)
                wgt[:, col] += jnp.sum(weighted.reshape(KT // 8, 8, tok), axis=0)
                probs.append((e * tot[0:1, col]).astype(jnp.bfloat16))
            dvs.append(dot(jnp.concatenate(probs, axis=1), gst[...], 1, 0))
        return jnp.concatenate(dvs, axis=0)

    def first_dp_step(i, carry):
        s = reach - i
        dsend[s - 1, 1] = first_dp(s).astype(jnp.bfloat16)
        copy_d(s, 1).start()
        return carry

    def take(kind, whole, stacked):
        local_a(kind).wait()
        for d in range(1, heads):
            arrival_a(kind, d).wait_recv()
        for j in range(GROUP):
            stacked[j * tok:(j + 1) * tok] = whole[:, j * HD:(j + 1) * HD]

    take(2, qs, qst)
    first(0, True)
    reach = jnp.minimum(pos, back)

    def first_step(masked, s, carry):
        for d in range(heads):
            copy_b(s, d).wait_recv()
        first(s, masked)
        return carry

    edge = jnp.minimum(reach, free)
    lax.fori_loop(1, edge + 1, functools.partial(first_step, False), 0)
    if back > free:
        lax.fori_loop(edge + 1, reach + 1, functools.partial(first_step, True), 0)
    inv = 1.0 / jnp.sum(tot[...], axis=0, keepdims=True)
    tot[0:1] = inv
    take(3, gs, gst)
    lax.fori_loop(0, reach, first_dp_step, 0)
    own[1] = first_dp(0)

    delta = jnp.sum(wgt[...], axis=0, keepdims=True) * tot[0:1]
    wgt[0:1] = delta

    def second(s):
        dks = []
        for t in range(tok // KT):
            at_t = slice(t * KT, (t + 1) * KT)
            scs = []
            for j in range(GROUP):
                col = slice(j * tok, (j + 1) * tok)
                capped = c_all[s, at_t, col]
                prob = e_all[s, at_t, col] * tot[0:1, col]
                diff = d_all[s, at_t, col].astype(jnp.float32) - wgt[0:1, col]
                scs.append(
                    (prob * diff * (QUERY_SCALE - QUERY_SCALE * (capped * capped))).astype(jnp.bfloat16)
                )
            scaled = jnp.concatenate(scs, axis=1)
            dks.append(dot(scaled, qst[...], 1, 0))
            dqt[...] += dot(kv[s, 0, at_t], scaled, 0, 0)
        return jnp.concatenate(dks, axis=0)

    def second_step(i, carry):
        s = reach - i
        dsend[s - 1, 0] = second(s).astype(jnp.bfloat16)
        copy_d(s, 0).start()
        return carry

    lax.fori_loop(0, reach, second_step, 0)
    own[0] = second(0)
    for j in range(GROUP):
        dq[:, j * HD:(j + 1) * HD] = dqt[:, j * tok:(j + 1) * tok].T.astype(jnp.bfloat16)

    outs = ((q_out, GROUP * HD), (k_out, HD), (v_out, HD))

    def src_e(kind, who):
        return dq.at[part(who)] if kind == 0 else dkv.at[kind - 1, part(who)]

    def copy_e(kind, d):
        ref, width = outs[kind]
        return pltpu.make_async_remote_copy(
            src_ref=src_e(kind, head_at(d)), dst_ref=ref.at[:, lanes(h, width)],
            send_sem=e_send.at[kind, d], recv_sem=e_recv.at[kind, d],
            device_id={"head": head_at(d)}, device_id_type=MESH,
        )

    def arrival_e(kind, d):
        ref, width = outs[kind]
        return pltpu.make_async_remote_copy(
            src_ref=src_e(kind, h), dst_ref=ref.at[:, lanes(head_at(heads - d), width)],
            send_sem=e_send.at[kind, d], recv_sem=e_recv.at[kind, d],
            device_id={"head": head_at(d)}, device_id_type=MESH,
        )

    def local_e(kind):
        ref, width = outs[kind]
        return pltpu.make_async_copy(src_e(kind, h), ref.at[:, lanes(h, width)], e_loc.at[kind])

    for d in range(1, heads):
        copy_e(0, d).start()
    local_e(0).start()

    def collect(s, carry):
        for which in (0, 1):
            copy_d(s, which).wait_recv()
        own[...] += drecv[s - 1].astype(jnp.float32)
        return carry

    lax.fori_loop(1, jnp.minimum(ctx - 1 - pos, back) + 1, collect, 0)
    dkv[...] = own[...].astype(jnp.bfloat16)
    for kind in (1, 2):
        for d in range(1, heads):
            copy_e(kind, d).start()
        local_e(kind).start()

    for kind in range(4):
        for d in range(1, heads):
            copy_a(kind, d).wait_send()

    def sent_b(s, carry):
        for d in range(heads):
            copy_b(s, d).wait_send()
        return carry

    lax.fori_loop(1, jnp.minimum(ctx - 1 - pos, back) + 1, sent_b, 0)

    def sent_d(s, carry):
        for which in (0, 1):
            copy_d(s, which).wait_send()
        return carry

    lax.fori_loop(1, reach + 1, sent_d, 0)
    for kind in range(3):
        local_e(kind).wait()
        for d in range(1, heads):
            copy_e(kind, d).wait_send()
            arrival_e(kind, d).wait_recv()


def hand_on(a, b, c, a_to, b_to, c_to, a_via, b_via, c_via, sems):
    ways = ((a, a_via, a_to), (b, b_via, b_to), (c, c_via, c_to))
    into = [pltpu.make_async_copy(x, v, sems.at[0, i]) for i, (x, v, _) in enumerate(ways)]
    out = [pltpu.make_async_copy(v, y, sems.at[1, i]) for i, (_, v, y) in enumerate(ways)]
    for copy in into:
        copy.start()
    for before, after in zip(into, out):
        before.wait()
        after.start()
    for copy in out:
        copy.wait()


def solution(mesh):
    heads, outer_n, inner_n = (mesh.shape[a] for a in ("head", "outer", "inner"))

    def body(query_in, key_in, value_in, grad_out):
        rows = query_in.shape[1]
        tok = rows * heads
        back = min((WINDOW + tok - 2) // tok, outer_n * inner_n - 1)
        wide = GROUP * tok
        bf16, f32 = jnp.bfloat16, jnp.float32
        sem = pltpu.SemaphoreType.DMA
        shapes = [(query_in.shape[1:]), (key_in.shape[1:]), (value_in.shape[1:])]
        res = pl.pallas_call(
            functools.partial(kernel, heads, outer_n, inner_n, back),
            out_shape=[jax.ShapeDtypeStruct(s, bf16) for s in shapes],
            in_specs=[pl.BlockSpec(memory_space=pl.ANY)] * 4,
            out_specs=[pl.BlockSpec(memory_space=pl.ANY)] * 3,
            scratch_shapes=[
                pltpu.VMEM((tok, GROUP * HD), bf16),
                pltpu.VMEM((tok, GROUP * HD), bf16),
                pltpu.VMEM((wide, HD), bf16),
                pltpu.VMEM((wide, HD), bf16),
                pltpu.VMEM((back + 1, 2, tok, HD), bf16),
                pltpu.VMEM((back + 1, tok, wide), f32),
                pltpu.VMEM((back + 1, tok, wide), f32),
                pltpu.VMEM((back + 1, tok, wide), bf16),
                pltpu.VMEM((8, wide), f32),
                pltpu.VMEM((8, wide), f32),
                pltpu.VMEM((tok, wide), bf16),
                pltpu.VMEM((tok, wide), bf16),
                pltpu.VMEM((HD, wide), f32),
                pltpu.VMEM((tok, GROUP * HD), bf16),
                pltpu.VMEM((2, tok, HD), bf16),
                pltpu.VMEM((back, 2, tok, HD), bf16),
                pltpu.VMEM((back, 2, tok, HD), bf16),
                pltpu.VMEM((2, tok, HD), f32),
                sem((4, heads)), sem((4, heads)), sem((4,)),
                sem((back + 1, heads)), sem((back + 1, heads)),
                sem((back, 2)), sem((back, 2)),
                sem((3, heads)), sem((3, heads)), sem((3,)),
            ],
            compiler_params=pltpu.CompilerParams(
                collective_id=0, has_side_effects=True, vmem_limit_bytes=60 * 1024 * 1024
            ),
        )(query_in[0], key_in[0], value_in[0], grad_out[0])
        res = pl.pallas_call(
            hand_on,
            out_shape=[jax.ShapeDtypeStruct(s, bf16) for s in shapes],
            in_specs=[pl.BlockSpec(memory_space=pl.ANY)] * 3,
            out_specs=[pl.BlockSpec(memory_space=pl.ANY)] * 3,
            scratch_shapes=[pltpu.VMEM(s, bf16) for s in shapes] + [sem((2, 3))],
        )(*res)
        return tuple(r[None] for r in res)

    spec = P(("outer", "inner"), "head", None)
    return jax.shard_map(
        body, mesh=mesh, in_specs=(spec,) * 4, out_specs=(spec,) * 3, check_vma=False
    )
```

```python
import functools

import jax
import jax.numpy as jnp
from jax import lax
from jax.experimental import pallas as pl
from jax.experimental.pallas import tpu as pltpu
from jax.sharding import PartitionSpec as P

HD = 128
GROUP = 2
WINDOW = 4096
SOFT_CAP = 50.0
QUERY_SCALE = 1.0 / 12.0
MESH = pl.DeviceIdType.MESH
KT = 128


def dot(a, b, ca, cb):
    return lax.dot_general(a, b, (((ca,), (cb,)), ((), ())), preferred_element_type=jnp.float32)


def kernel(
    heads, outer_n, inner_n, back,
    q_in, k_in, v_in, g_in,
    q_out, k_out, v_out,
    qs, gs, qst, gst, kv, e_all, c_all, d_all, tot, wgt, pb, sc, dqt, dq, dkv, dsend, drecv, own,
    a_send, a_recv, a_loc, b_send, b_recv, d_ssem, d_rsem, e_send, e_recv, e_loc,
):
    rows = q_in.shape[0]
    tok = rows * heads
    ctx = outer_n * inner_n
    h = lax.axis_index("head")
    pos = lax.axis_index("outer") * inner_n + lax.axis_index("inner")

    def at(t):
        return {"outer": lax.div(t, inner_n), "inner": lax.rem(t, inner_n)}

    def head_at(d):
        return lax.rem(h + d, heads)

    def part(who):
        return pl.ds(pl.multiple_of(who * rows, rows), rows)

    def lanes(who, width):
        return pl.ds(pl.multiple_of(who * width, width), width)

    barrier = pltpu.get_barrier_semaphore()
    for d in range(1, heads):
        pl.semaphore_signal(barrier, inc=1, device_id={"head": head_at(d)}, device_id_type=MESH)
    for s in range(1, back + 1):
        @pl.when(pos + s < ctx)
        def _():
            pl.semaphore_signal(barrier, inc=1, device_id=at(pos + s), device_id_type=MESH)

        @pl.when(pos - s >= 0)
        def _():
            pl.semaphore_signal(barrier, inc=1, device_id=at(pos - s), device_id_type=MESH)
    peers = heads - 1 + jnp.minimum(pos, back) + jnp.minimum(ctx - 1 - pos, back)
    pl.semaphore_wait(barrier, peers)

    srcs = ((k_in, HD), (v_in, HD), (q_in, GROUP * HD), (g_in, GROUP * HD))

    def dst_a(kind, who):
        if kind < 2:
            return kv.at[0, kind, part(who)]
        return (qs if kind == 2 else gs).at[part(who)]

    def copy_a(kind, d):
        ref, width = srcs[kind]
        return pltpu.make_async_remote_copy(
            src_ref=ref.at[:, lanes(head_at(d), width)],
            dst_ref=dst_a(kind, h),
            send_sem=a_send.at[kind, d], recv_sem=a_recv.at[kind, d],
            device_id={"head": head_at(d)}, device_id_type=MESH,
        )

    def arrival_a(kind, d):
        ref, width = srcs[kind]
        return pltpu.make_async_remote_copy(
            src_ref=ref.at[:, lanes(h, width)],
            dst_ref=dst_a(kind, head_at(heads - d)),
            send_sem=a_send.at[kind, d], recv_sem=a_recv.at[kind, d],
            device_id={"head": head_at(d)}, device_id_type=MESH,
        )

    def local_a(kind):
        ref, width = srcs[kind]
        return pltpu.make_async_copy(ref.at[:, lanes(h, width)], dst_a(kind, h), a_loc.at[kind])

    for kind in (0, 1):
        local_a(kind).start()
    for kind in (0, 1, 2, 3):
        for d in range(1, heads):
            copy_a(kind, d).start()
    for kind in (2, 3):
        local_a(kind).start()

    def copy_b(s, d):
        who = part(head_at(heads - d))
        return pltpu.make_async_remote_copy(
            src_ref=kv.at[0, :, who], dst_ref=kv.at[s, :, who],
            send_sem=b_send.at[s, d], recv_sem=b_recv.at[s, d],
            device_id=at(lax.rem(pos + s, ctx)), device_id_type=MESH,
        )

    for d in range(heads):
        for kind in (0, 1):
            if d == 0:
                local_a(kind).wait()
            else:
                arrival_a(kind, d).wait_recv()
        for s in range(1, back + 1):
            @pl.when(pos + s < ctx)
            def _():
                copy_b(s, d).start()

    tot[...] = jnp.zeros_like(tot)
    wgt[...] = jnp.zeros_like(wgt)
    dqt[...] = jnp.zeros_like(dqt)

    free = (WINDOW - tok) // tok

    def first(s, masked):
        for t in range(tok // KT):
            at_t = slice(t * KT, (t + 1) * KT)
            keys = kv[s, 0, at_t]
            for j in range(GROUP):
                col = slice(j * tok, (j + 1) * tok)
                capped = jnp.tanh(dot(keys, qst[col], 1, 1) * (QUERY_SCALE / SOFT_CAP))
                e = jnp.exp(SOFT_CAP * capped)
                if masked:
                    apart = (
                        s * tok - t * KT
                        + lax.broadcasted_iota(jnp.int32, e.shape, 1)
                        - lax.broadcasted_iota(jnp.int32, e.shape, 0)
                    )
                    e = jnp.where((apart >= 0) & (apart < WINDOW), e, 0.0)
                c_all[s, at_t, col] = capped
                e_all[s, at_t, col] = e
                tot[:, col] += jnp.sum(e.reshape(KT // 8, 8, tok), axis=0)

    def copy_d(s, which):
        return pltpu.make_async_remote_copy(
            src_ref=dsend.at[s - 1, which], dst_ref=drecv.at[s - 1, which],
            send_sem=d_ssem.at[s - 1, which], recv_sem=d_rsem.at[s - 1, which],
            device_id=at(lax.rem(pos - s + ctx, ctx)), device_id_type=MESH,
        )

    def first_dp(s):
        dvs = []
        for t in range(tok // KT):
            at_t = slice(t * KT, (t + 1) * KT)
            vals = kv[s, 1, at_t]
            probs = []
            for j in range(GROUP):
                col = slice(j * tok, (j + 1) * tok)
                dp = dot(vals, gst[col], 1, 1).astype(jnp.bfloat16)
                d_all[s, at_t, col] = dp
                e = e_all[s, at_t, col]
                weighted = e * dp.astype(jnp.float32)
                wgt[:, col] += jnp.sum(weighted.reshape(KT // 8, 8, tok), axis=0)
                probs.append((e * tot[0:1, col]).astype(jnp.bfloat16))
            dvs.append(dot(jnp.concatenate(probs, axis=1), gst[...], 1, 0))
        return jnp.concatenate(dvs, axis=0)

    def first_dp_step(i, carry):
        s = reach - i
        dsend[s - 1, 1] = first_dp(s).astype(jnp.bfloat16)
        copy_d(s, 1).start()
        return carry

    def take(kind, whole, stacked):
        local_a(kind).wait()
        for d in range(1, heads):
            arrival_a(kind, d).wait_recv()
        for j in range(GROUP):
            stacked[j * tok:(j + 1) * tok] = whole[:, j * HD:(j + 1) * HD]

    take(2, qs, qst)
    first(0, True)
    reach = jnp.minimum(pos, back)

    def first_step(masked, s, carry):
        for d in range(heads):
            copy_b(s, d).wait_recv()
        first(s, masked)
        return carry

    edge = jnp.minimum(reach, free)
    lax.fori_loop(1, edge + 1, functools.partial(first_step, False), 0)
    if back > free:
        lax.fori_loop(edge + 1, reach + 1, functools.partial(first_step, True), 0)
    inv = 1.0 / jnp.sum(tot[...], axis=0, keepdims=True)
    tot[0:1] = inv
    take(3, gs, gst)
    lax.fori_loop(0, reach, first_dp_step, 0)
    own[1] = first_dp(0)

    delta = jnp.sum(wgt[...], axis=0, keepdims=True) * tot[0:1]
    wgt[0:1] = delta

    def second(s):
        dks = []
        for t in range(tok // KT):
            at_t = slice(t * KT, (t + 1) * KT)
            scs = []
            for j in range(GROUP):
                col = slice(j * tok, (j + 1) * tok)
                capped = c_all[s, at_t, col]
                prob = e_all[s, at_t, col] * tot[0:1, col]
                diff = d_all[s, at_t, col].astype(jnp.float32) - wgt[0:1, col]
                scs.append(
                    (prob * diff * (QUERY_SCALE - QUERY_SCALE * (capped * capped))).astype(jnp.bfloat16)
                )
            scaled = jnp.concatenate(scs, axis=1)
            dks.append(dot(scaled, qst[...], 1, 0))
            dqt[...] += dot(kv[s, 0, at_t], scaled, 0, 0)
        return jnp.concatenate(dks, axis=0)

    def second_step(i, carry):
        s = reach - i
        dsend[s - 1, 0] = second(s).astype(jnp.bfloat16)
        copy_d(s, 0).start()
        return carry

    lax.fori_loop(0, reach, second_step, 0)
    own[0] = second(0)
    for j in range(GROUP):
        dq[:, j * HD:(j + 1) * HD] = dqt[:, j * tok:(j + 1) * tok].T.astype(jnp.bfloat16)

    outs = ((q_out, GROUP * HD), (k_out, HD), (v_out, HD))

    def src_e(kind, who):
        return dq.at[part(who)] if kind == 0 else dkv.at[kind - 1, part(who)]

    def copy_e(kind, d):
        ref, width = outs[kind]
        return pltpu.make_async_remote_copy(
            src_ref=src_e(kind, head_at(d)), dst_ref=ref.at[:, lanes(h, width)],
            send_sem=e_send.at[kind, d], recv_sem=e_recv.at[kind, d],
            device_id={"head": head_at(d)}, device_id_type=MESH,
        )

    def arrival_e(kind, d):
        ref, width = outs[kind]
        return pltpu.make_async_remote_copy(
            src_ref=src_e(kind, h), dst_ref=ref.at[:, lanes(head_at(heads - d), width)],
            send_sem=e_send.at[kind, d], recv_sem=e_recv.at[kind, d],
            device_id={"head": head_at(d)}, device_id_type=MESH,
        )

    def local_e(kind):
        ref, width = outs[kind]
        return pltpu.make_async_copy(src_e(kind, h), ref.at[:, lanes(h, width)], e_loc.at[kind])

    for d in range(1, heads):
        copy_e(0, d).start()
    local_e(0).start()

    def collect(which, s, carry):
        copy_d(s, which).wait_recv()
        own[which] += drecv[s - 1, which].astype(jnp.float32)
        return carry

    for which in (1, 0):
        later = jnp.minimum(ctx - 1 - pos, back)
        lax.fori_loop(1, later + 1, functools.partial(collect, which), 0)
        dkv[which] = own[which].astype(jnp.bfloat16)
        for d in range(1, heads):
            copy_e(which + 1, d).start()
        local_e(which + 1).start()

    for kind in range(4):
        for d in range(1, heads):
            copy_a(kind, d).wait_send()

    def sent_b(s, carry):
        for d in range(heads):
            copy_b(s, d).wait_send()
        return carry

    lax.fori_loop(1, jnp.minimum(ctx - 1 - pos, back) + 1, sent_b, 0)

    def sent_d(s, carry):
        for which in (0, 1):
            copy_d(s, which).wait_send()
        return carry

    lax.fori_loop(1, reach + 1, sent_d, 0)
    for kind in range(3):
        local_e(kind).wait()
        for d in range(1, heads):
            copy_e(kind, d).wait_send()
            arrival_e(kind, d).wait_recv()


def hand_on(a, b, c, a_to, b_to, c_to, a_via, b_via, c_via, sems):
    ways = ((a, a_via, a_to), (b, b_via, b_to), (c, c_via, c_to))
    into = [pltpu.make_async_copy(x, v, sems.at[0, i]) for i, (x, v, _) in enumerate(ways)]
    out = [pltpu.make_async_copy(v, y, sems.at[1, i]) for i, (_, v, y) in enumerate(ways)]
    for copy in into:
        copy.start()
    for before, after in zip(into, out):
        before.wait()
        after.start()
    for copy in out:
        copy.wait()


def solution(mesh):
    heads, outer_n, inner_n = (mesh.shape[a] for a in ("head", "outer", "inner"))

    def body(query_in, key_in, value_in, grad_out):
        rows = query_in.shape[1]
        tok = rows * heads
        back = min((WINDOW + tok - 2) // tok, outer_n * inner_n - 1)
        wide = GROUP * tok
        bf16, f32 = jnp.bfloat16, jnp.float32
        sem = pltpu.SemaphoreType.DMA
        shapes = [(query_in.shape[1:]), (key_in.shape[1:]), (value_in.shape[1:])]
        res = pl.pallas_call(
            functools.partial(kernel, heads, outer_n, inner_n, back),
            out_shape=[jax.ShapeDtypeStruct(s, bf16) for s in shapes],
            in_specs=[pl.BlockSpec(memory_space=pl.ANY)] * 4,
            out_specs=[pl.BlockSpec(memory_space=pl.ANY)] * 3,
            scratch_shapes=[
                pltpu.VMEM((tok, GROUP * HD), bf16),
                pltpu.VMEM((tok, GROUP * HD), bf16),
                pltpu.VMEM((wide, HD), bf16),
                pltpu.VMEM((wide, HD), bf16),
                pltpu.VMEM((back + 1, 2, tok, HD), bf16),
                pltpu.VMEM((back + 1, tok, wide), f32),
                pltpu.VMEM((back + 1, tok, wide), f32),
                pltpu.VMEM((back + 1, tok, wide), bf16),
                pltpu.VMEM((8, wide), f32),
                pltpu.VMEM((8, wide), f32),
                pltpu.VMEM((tok, wide), bf16),
                pltpu.VMEM((tok, wide), bf16),
                pltpu.VMEM((HD, wide), f32),
                pltpu.VMEM((tok, GROUP * HD), bf16),
                pltpu.VMEM((2, tok, HD), bf16),
                pltpu.VMEM((back, 2, tok, HD), bf16),
                pltpu.VMEM((back, 2, tok, HD), bf16),
                pltpu.VMEM((2, tok, HD), f32),
                sem((4, heads)), sem((4, heads)), sem((4,)),
                sem((back + 1, heads)), sem((back + 1, heads)),
                sem((back, 2)), sem((back, 2)),
                sem((3, heads)), sem((3, heads)), sem((3,)),
            ],
            compiler_params=pltpu.CompilerParams(
                collective_id=0, has_side_effects=True, vmem_limit_bytes=60 * 1024 * 1024
            ),
        )(query_in[0], key_in[0], value_in[0], grad_out[0])
        res = pl.pallas_call(
            hand_on,
            out_shape=[jax.ShapeDtypeStruct(s, bf16) for s in shapes],
            in_specs=[pl.BlockSpec(memory_space=pl.ANY)] * 3,
            out_specs=[pl.BlockSpec(memory_space=pl.ANY)] * 3,
            scratch_shapes=[pltpu.VMEM(s, bf16) for s in shapes] + [sem((2, 3))],
        )(*res)
        return tuple(r[None] for r in res)

    spec = P(("outer", "inner"), "head", None)
    return jax.shard_map(
        body, mesh=mesh, in_specs=(spec,) * 4, out_specs=(spec,) * 3, check_vma=False
    )
```
